32 devices in a mesh: groups: 2 (over y), tm: 16 (over z, x, core).
Axes of the slice: x: 2, y: 2, z: 4, core: 2. Of those that a mesh axis runs over, the one named last changes fastest.
Arguments:
- start_frames: float32 [6, 4, 8, 256], P('groups'), parts along dimension 0, may hold values from -6 to 6
- plan: int32 [32], P(('groups', 'tm')), parts along dimension 0, may hold values from 0 to 999
- noise: float32 [16, 6, 4, 8, 256], P('tm', 'groups'), parts along dimension 1, may hold values from -6 to 6
- w_lift: float32 [3, 128], replicated, may hold values from -3.5 to 3.5
- w_time: float32 [128, 128], replicated, may hold values from -0.75 to 0.75
- spatial: float32 [2, 128, 9], replicated, may hold values from -2 to 2
- temporal: float32 [2, 128, 3], replicated, may hold values from -3.5 to 3.5
- w_point: bfloat16 [2, 128, 128], replicated, may hold values from -0.5 to 0.5
- w_out: float32 [128, 3], replicated, may hold values from -0.5 to 0.5
Outputs:
- trajectory: float32 [16, 6, 4, 8, 256], P('tm', 'groups'), parts along dimension 1
The draws below stay inside these ranges and needn't reach their ends.
There are 2 independent parts, one for each index of `groups`. The reference program is written for one: setup_inputs(seed, part) draws one part's arguments, and reference() takes and returns one part's arrays. A program takes and returns all parts, laid end to end along the dimension named above; an argument that names none is the same for every part. Nothing has to cross between parts.
All inputs are finite; a program needn't handle non-finite values.
Results may differ from the reference program's by a relative error of at most 0.0023.
Values sent between devices are 32-bit elements; how exact they have to be, the bound alone decides.
A program may use at most 64 MiB of HBM per device.

```python
import math
import jax
import jax.numpy as jnp
from jax import lax

C = 3
HID = 128
F = 4
H = 8
W = 256
ITERS = 2
BLOCKS = 2
TIMES = 16


def touch_ends(entries, key, smallest, high):
    longest = entries.shape.index(max(entries.shape))
    spots = []
    for shift in (0, 1):
        where = [jax.random.randint(jax.random.fold_in(key, axis), (), 0, length) for axis, length in enumerate(entries.shape)]
        where[longest] = (where[longest] + shift) % entries.shape[longest]
        spots.append(tuple(where))
    return entries.at[spots[0]].set(smallest).at[spots[1]].set(high)


def block_scale(own_key, extent, cuts, least, largest):
    def one(position, parts):
        draws = jax.random.uniform(jax.random.fold_in(jax.random.fold_in(own_key, 6), position), (parts,), jnp.float32, least / len(cuts), largest / len(cuts))
        return jnp.repeat(jnp.exp(draws), extent[position] // parts).reshape((-1,) + (1,) * (len(extent) - position - 1))

    gain = one(*cuts[0])
    for cut in cuts[1:]:
        gain = gain * one(*cut)
    return gain


def normal_values(rng, extent, scale, limit, cuts=(), held_as=jnp.bfloat16):
    values = scale * jax.random.normal(rng, extent, jnp.float32)
    if cuts:
        values = values * block_scale(rng, extent, cuts, -0.22, 0.18)
    return jnp.clip(values, -limit, limit).astype(held_as)


def setup_inputs(seed: int = 0, part: int = 0) -> dict:
    seeds = jax.random.split(jax.random.key(seed), 10)
    part_splits = jax.random.split(jax.random.fold_in(seeds[9], part), 10)
    start_frames = normal_values(part_splits[0], (C, F, H, W), 1.0, 6.0, (), jnp.float32)
    plan = touch_ends(jax.random.randint(part_splits[1], (TIMES,), 0, 1000), jax.random.fold_in(part_splits[1], 1), 0, 999).astype(jnp.int32)
    noise = normal_values(part_splits[2], (TIMES, C, F, H, W), 1.0, 6.0, ((0, 16),), jnp.float32)
    w_lift = normal_values(seeds[3], (C, HID), C ** -0.5, 3.5, (), jnp.float32)
    w_time = normal_values(seeds[4], (HID, HID), (HID // 2) ** -0.5, 0.75, (), jnp.float32)
    spatial = normal_values(seeds[5], (BLOCKS, HID, 9), 9 ** -0.5, 2.0, (), jnp.float32)
    temporal = normal_values(seeds[6], (BLOCKS, HID, 3), 3 ** -0.5, 3.5, (), jnp.float32)
    w_point = normal_values(seeds[7], (BLOCKS, HID, HID), HID ** -0.5, 0.5)
    w_out = normal_values(seeds[8], (HID, C), HID ** -0.5, 0.5, (), jnp.float32)
    return {"start_frames": start_frames, "plan": plan, "noise": noise, "w_lift": w_lift, "w_time": w_time, "spatial": spatial, "temporal": temporal, "w_point": w_point, "w_out": w_out}


noise_scale = 2.0

def embedding(step_index, width):
    half_width = width // 2
    column = jnp.arange(half_width, dtype=jnp.float32)
    freqs = jnp.exp(-math.log(1000.0) * column / half_width)
    angles = step_index.astype(jnp.float32) * freqs
    return jnp.concatenate([jnp.sin(angles), jnp.cos(angles)])

def convolve(values, kernel_space, kernel_time):
    frames, rows, columns = (values.shape[1], values.shape[2], values.shape[3])
    padded = jnp.pad(values, ((0, 0), (0, 0), (1, 1), (1, 1)))
    spatial_sum = jnp.zeros_like(values)
    for row_tap in range(3):
        for col_tap in range(3):
            spatial_sum = spatial_sum + kernel_space[:, 3 * row_tap + col_tap, None, None, None] * padded[:, :, row_tap:row_tap + rows, col_tap:col_tap + columns]
    framed = jnp.pad(spatial_sum, ((0, 0), (1, 1), (0, 0), (0, 0)))
    result = jnp.zeros_like(values)
    for frame_tap in range(3):
        result = result + kernel_time[:, frame_tap, None, None, None] * framed[:, frame_tap:frame_tap + frames]
    return result

def network(states, step_index, w_lift, w_time, spatial, temporal, w_point, w_out):
    width = w_time.shape[0]
    shape_cells = states.shape[1:]
    bias = jnp.dot(embedding(step_index, width), w_time, precision=lax.Precision.HIGHEST)
    flat_states = states.reshape(states.shape[0], -1)
    lifted = jnp.dot(w_lift.T, flat_states, precision=lax.Precision.HIGHEST) + bias[:, None]
    features = lifted.astype(jnp.bfloat16)
    for block in range(spatial.shape[0]):
        mixed = convolve(features.astype(jnp.float32).reshape((width,) + shape_cells), spatial[block], temporal[block]).reshape(width, -1)
        root_mean = jnp.sqrt(lax.optimization_barrier(jnp.mean(mixed * mixed, axis=0, keepdims=True)) + 1e-06)
        normed = jax.nn.silu(mixed / root_mean).astype(jnp.bfloat16)
        update = jnp.dot(w_point[block].T, normed, preferred_element_type=jnp.float32)
        features = (features.astype(jnp.float32) + update).astype(jnp.bfloat16)
    output = jnp.dot(w_out.T, features.astype(jnp.float32), precision=lax.Precision.HIGHEST)
    return output.reshape(states.shape)

def reference(start_frames, plan, noise, w_lift, w_time, spatial, temporal, w_point, w_out):
    step_size = 1.0 / TIMES

    def drift_of(items):
        states, step_index, noise_now = items
        value = network(states, step_index, w_lift, w_time, spatial, temporal, w_point, w_out)
        return step_size * value + noise_scale * math.sqrt(step_size) * noise_now
    states_all = jnp.broadcast_to(start_frames[None], noise.shape)
    result = states_all
    for iteration in range(ITERS):
        drifts = lax.map(drift_of, (states_all, plan, noise))
        running = jnp.cumsum(drifts, axis=0)
        if iteration + 1 < ITERS:
            before = jnp.concatenate([jnp.zeros_like(drifts[:1]), running[:-1]], axis=0)
            states_all = start_frames[None] + before
        else:
            result = start_frames[None] + running
    return result
```

```python
import functools
import math

import jax
import jax.numpy as jnp
from jax import lax
from jax.experimental import pallas as pl
from jax.experimental.pallas import tpu as pltpu
from jax.sharding import PartitionSpec as P

ITERS = 2
NOISE_SCALE = 2.0
MESH = pl.DeviceIdType.MESH
LANES = 128
STRIPS = 16
TILE = 16
NT = (((1,), (1,)), ((), ()))


def split_bf16(value):
    high = value.astype(jnp.bfloat16)
    return high, (value - high.astype(jnp.float32)).astype(jnp.bfloat16)


def kernel(
    n, quad, dims,
    plan_ref, start_hbm, noise_hbm, lift_hbm, time_hbm, spatial_hbm, temporal_hbm, point_hbm, wout_hbm,
    out_ref,
    start, noise, lift_in, time_in, spatial_in, temporal_in, point_in, wout_in,
    lift_w, out_w, state, sent, near, total, far, before, final,
    in_sem, send_sem, recv_sem,
    feat_a, feat_b, last, time_a, time_b, pend, normed, place, taps, point_w, mean_w, lift_b, out_b,
):
    channels, frames, rows, width, hid, blocks = dims
    halves = width // LANES
    planes = channels * frames
    strip = width // STRIPS
    cells = strip * STRIPS
    levels = n // quad
    step_size = 1.0 / n
    bf16 = jnp.bfloat16
    me = lax.axis_index("tm")
    level, member = lax.div(me, quad), lax.rem(me, quad)

    loads = [
        (start_hbm.at[:, pl.ds(half * LANES, LANES)], start.at[half]) for half in range(halves)
    ]
    loads += [(lift_hbm, lift_in), (time_hbm, time_in), (spatial_hbm, spatial_in)]
    loads += [(temporal_hbm, temporal_in), (point_hbm, point_in), (wout_hbm, wout_in)]
    loads += [
        (noise_hbm.at[:, pl.ds(half * LANES, LANES)], noise.at[half]) for half in range(halves)
    ]
    loads = [
        pltpu.make_async_copy(source, target, in_sem.at[k])
        for k, (source, target) in enumerate(loads)
    ]
    for load in loads:
        load.start()

    barrier = pltpu.get_barrier_semaphore()

    @pl.loop(1, n)
    def _(k):
        pl.semaphore_signal(
            barrier, inc=1, device_id={"tm": lax.rem(me + k, n)}, device_id_type=MESH
        )

    for feat in (time_a, time_b):
        for frame in range(frames):
            for row in (0, rows + 1):
                feat[frame, row] = jnp.zeros((strip + 2, STRIPS, hid), bf16)
    spot = lax.broadcasted_iota(jnp.int32, ((strip + 2) * STRIPS, width), 0)
    column = lax.broadcasted_iota(jnp.int32, ((strip + 2) * STRIPS, width), 1)
    wanted = lax.rem(spot, STRIPS) * strip + lax.div(spot, STRIPS) - 1
    place[...] = jnp.where(column == wanted, 1.0, 0.0).astype(bf16)
    one_row = lax.broadcasted_iota(jnp.int32, (rows, TILE, width), 1) == planes
    state[...] = jnp.where(one_row, 1.0, 0.0)
    lift_w[...] = jnp.zeros_like(lift_w)
    out_w[...] = jnp.zeros_like(out_w)
    mean_w[...] = jnp.zeros_like(mean_w)
    point_w[...] = jnp.zeros_like(point_w)
    for out in range(2):
        here = slice(out * hid, (out + 1) * hid)
        mean_w[here, here] = jnp.full((hid, hid), 4.0 / hid, bf16)

    lane = lax.broadcasted_iota(jnp.int32, (8, hid), 1)
    half_hid = hid // 2
    index = lax.rem(lane, half_hid).astype(jnp.float32)
    angles = plan_ref[0].astype(jnp.float32) * jnp.exp(-math.log(1000.0) * index / half_hid)
    embedded = jnp.where(lane < half_hid, jnp.sin(angles), jnp.cos(angles))

    for load in loads:
        load.wait()

    bias = jnp.dot(
        embedded, time_in[...], precision=lax.Precision.HIGHEST, preferred_element_type=jnp.float32
    )[0:1]

    def split_rows(rows_value):
        high = rows_value.astype(bf16).astype(jnp.float32)
        return high, rows_value - high

    bias_high, bias_low = split_rows(bias)
    lift_high, lift_low = split_rows(lift_in[...])
    out_high, out_low = split_rows(wout_in[...])
    for frame in range(frames):
        here = slice(frame * hid, (frame + 1) * hid)
        for channel in range(channels):
            k = channel * frames + frame
            lift_w[k : k + 1, here] = lift_high[channel : channel + 1]
            lift_w[TILE + k : TILE + k + 1, here] = lift_high[channel : channel + 1]
            lift_w[2 * TILE + k : 2 * TILE + k + 1, here] = lift_low[channel : channel + 1]
            out_w[k : k + 1, here] = out_high[channel : channel + 1]
            out_w[TILE + k : TILE + k + 1, here] = out_low[channel : channel + 1]
        lift_w[planes : planes + 1, here] = bias_high
        lift_w[2 * TILE + planes : 2 * TILE + planes + 1, here] = bias_low
    lift_b[...] = lift_w[...].astype(bf16)
    out_b[...] = out_w[...].astype(bf16)
    for block in range(blocks):
        for out in range(2):
            here = slice(out * hid, (out + 1) * hid)
            point_w[block, here, here] = point_in[block]
        for k in range(9):
            weight = spatial_in[k, block : block + 1, :]
            taps[block, k] = jnp.broadcast_to(weight, (STRIPS, hid)).astype(bf16)
        for k in range(3):
            weight = temporal_in[k, block : block + 1, :]
            taps[block, 9 + k] = jnp.broadcast_to(weight, (STRIPS, hid)).astype(bf16)

    def quad_copy(it, row, k):
        return pltpu.make_async_remote_copy(
            src_ref=sent.at[it, row], dst_ref=near.at[it, row, member],
            send_sem=send_sem.at[it, row, k], recv_sem=recv_sem.at[it, row, member],
            device_id={"tm": level * quad + lax.rem(member + k, quad)}, device_id_type=MESH,
        )

    def quad_from(it, row, k):
        other = lax.rem(member + k, quad)
        return pltpu.make_async_remote_copy(
            src_ref=sent.at[it, row], dst_ref=near.at[it, row, other],
            send_sem=send_sem.at[it, row, k], recv_sem=recv_sem.at[it, row, other],
            device_id={"tm": level * quad + other}, device_id_type=MESH,
        )

    def level_copy(it, row, k):
        return pltpu.make_async_remote_copy(
            src_ref=total.at[it, row], dst_ref=far.at[it, row, level],
            send_sem=send_sem.at[it, row, quad + k], recv_sem=recv_sem.at[it, row, quad + level],
            device_id={"tm": me + k * quad}, device_id_type=MESH,
        )

    def level_from(it, row, lower):
        return pltpu.make_async_remote_copy(
            src_ref=total.at[it, row], dst_ref=far.at[it, row, lower],
            send_sem=send_sem.at[it, row, quad], recv_sem=recv_sem.at[it, row, quad + lower],
            device_id={"tm": lower * quad + member}, device_id_type=MESH,
        )

    def send(it, row):
        @pl.loop(1, quad)
        def _(k):
            quad_copy(it, row, k).start()

    def forward(it, row):
        near[it, row, member] = sent[it, row]

        @pl.loop(1, quad)
        def _(k):
            quad_from(it, row, k).wait_recv()

        zero = jnp.zeros((halves * planes, LANES), jnp.float32)
        everything, prefix = zero, zero
        for k in range(quad):
            part = near[it, row, k]
            everything = everything + part
            prefix = prefix + jnp.where(k < member, part, 0.0)
        total[it, row] = everything
        before[it, row] = prefix

        @pl.loop(1, levels - level)
        def _(k):
            level_copy(it, row, k).start()

    def arrive(it, row):
        @pl.loop(0, level)
        def _(lower):
            level_from(it, row, lower).wait_recv()
            before[it, row] += far[it, row, lower]

    def lift(it, row, target, at_row, blend, to_row):
        for half in range(halves):
            now = start[half, pl.ds(row, planes, stride=rows), :]
            if it > 0:
                now = now + before[it - 1, row, half * planes : (half + 1) * planes]
            state[row, 0:planes, half * LANES : (half + 1) * LANES] = now
        high, low = split_bf16(state[row])
        spare = jnp.zeros((LANES - 3 * TILE, width), bf16)
        stack = jnp.concatenate([high, low, high, spare], axis=0)
        turned = lax.dot_general(place[...], stack, NT, preferred_element_type=jnp.float32)
        lifted = jnp.dot(
            turned.astype(bf16), lift_b[...], preferred_element_type=jnp.float32
        ).astype(bf16)
        fresh = [
            lifted[:, frame * hid : (frame + 1) * hid].reshape(strip + 2, STRIPS, hid)
            for frame in range(frames)
        ]
        for frame in range(frames):
            target[frame, at_row] = fresh[frame][1 : strip + 1]
            blend[frame, to_row] = in_time(fresh, frame, 0)

    def in_time(fresh, frame, block):
        mixed = taps[block, 10] * fresh[frame]
        if frame > 0:
            mixed = mixed + taps[block, 9] * fresh[frame - 1]
        if frame + 1 < frames:
            mixed = mixed + taps[block, 11] * fresh[frame + 1]
        return mixed

    def convolve(source, first, block):
        weights = [taps[block, k] for k in range(9)]
        for frame in range(frames):
            for at in range(strip):
                lines = []
                for a in range(3):
                    terms = [weights[3 * a + c] * source[frame, first + a, at + c] for c in range(3)]
                    lines.append(terms[0] + terms[1] + terms[2])
                pend[frame, at] = lines[0] + lines[1] + lines[2]

    def pairs(ref):
        return jnp.concatenate(
            [
                jnp.concatenate([ref[pair + k].reshape(cells, hid) for k in range(2)], axis=1)
                for pair in range(0, frames, 2)
            ],
            axis=0,
        )

    def normalize():
        mixed = pairs(pend)
        mean = jnp.dot(mixed * mixed, mean_w[...], preferred_element_type=jnp.float32)
        scale = lax.rsqrt(mean.astype(bf16) + jnp.bfloat16(4e-06))
        half = mixed * scale
        done = half * jnp.tanh(half) + half
        for frame in range(frames):
            first, side = (frame // 2) * cells, (frame % 2) * hid
            part = done[first : first + cells, side : side + hid]
            normed[frame] = part.reshape(strip, STRIPS, hid)

    def update(source, at_row, target, to_row, block, blend=None, blend_row=None):
        sub = lax.broadcasted_iota(jnp.int32, (STRIPS, hid), 0)
        change = jnp.dot(pairs(normed), point_w[block], preferred_element_type=jnp.float32)
        fresh = []
        for frame in range(frames):
            first, side = (frame // 2) * cells, (frame % 2) * hid
            old = source[frame, at_row].reshape(cells, hid)
            now = old + change[first : first + cells, side : side + hid].astype(bf16)
            fresh.append(now.reshape(strip, STRIPS, hid))
            target[frame, to_row] = fresh[frame]
        if blend is None:
            return
        for frame in range(frames):
            mixed = in_time(fresh, frame, block + 1)
            blend[frame, blend_row, 1 : strip + 1] = mixed
            tail = mixed[strip - 1].astype(jnp.float32)
            tail = jnp.where(sub == 0, 0.0, pltpu.roll(tail, 1, 0))
            blend[frame, blend_row, 0] = tail.astype(bf16)
            head = mixed[0].astype(jnp.float32)
            head = jnp.where(sub == STRIPS - 1, 0.0, pltpu.roll(head, STRIPS - 1, 0))
            blend[frame, blend_row, strip + 1] = head.astype(bf16)

    def output(it, row, source, at_row):
        seen = jnp.concatenate(
            [source[frame, at_row].reshape(cells, hid) for frame in range(frames)], axis=1
        )
        both = lax.dot_general(out_b[...], seen, NT, preferred_element_type=jnp.float32)
        high, low = split_bf16(both[0:TILE] + both[TILE : 2 * TILE])
        turned = jnp.dot(
            jnp.concatenate([high, low], axis=0), place[STRIPS : STRIPS + cells, :],
            preferred_element_type=jnp.float32,
        )
        turned = turned[0:TILE] + turned[TILE : 2 * TILE]
        for half in range(halves):
            drift = (
                step_size * turned[0:planes, half * LANES : (half + 1) * LANES]
                + NOISE_SCALE
                * math.sqrt(step_size)
                * noise[half, pl.ds(row, planes, stride=rows), :]
            )
            sent[it, row, half * planes : (half + 1) * planes] = drift

    def step(it, v):
        if 0 <= v - 3 - rows < rows:
            output(it, v - 3 - rows, last, v - 3 - rows)
        if 0 <= v - 2 < rows:
            update(feat_a, v - 2, feat_b, v - 2, 0, time_b, v - 1)
        elif rows <= v - 2 < 2 * rows:
            update(feat_b, v - 2 - rows, last, v - 2 - rows, 1)
        if 0 <= v - 1 < 2 * rows:
            normalize()
        if v < rows:
            convolve(time_a, v, 0)
        elif v < 2 * rows:
            convolve(time_b, v - rows, 1)
        if v + 2 < rows:
            lift(it, v + 2, feat_a, v + 2, time_a, v + 3)

    for it in range(ITERS):
        for row in range(2):
            if it > 0:
                arrive(it - 1, row)
            lift(it, row, feat_a, row, time_a, row + 1)
        for v in range(2):
            if it > 0:
                arrive(it - 1, v + 2)
            step(it, v)

        @pl.loop(2, rows - 2)
        def _(v):
            if it > 0:
                arrive(it - 1, v + 2)
            plain = feat_a.at[:, pl.ds(v - 2, 5)]
            mixed = time_a.at[:, pl.ds(v, 4)]
            update(plain, 0, feat_b.at[:, pl.ds(v - 2, 1)], 0, 0, time_b.at[:, pl.ds(v - 1, 1)], 0)
            normalize()
            convolve(mixed, 0, 0)
            lift(it, v + 2, plain, 4, mixed, 3)

        for v in range(rows - 2, rows + 3):
            step(it, v)
        if it == 0:
            pl.semaphore_wait(barrier, n - 1)

        @pl.loop(rows + 3, 2 * rows)
        def _(v):
            row = v - rows
            seen = last.at[:, pl.ds(row - 3, 2)]
            output(it, row - 3, seen, 0)
            update(feat_b.at[:, pl.ds(row - 2, 1)], 0, seen, 1, 1)
            normalize()
            convolve(time_b.at[:, pl.ds(row, 3)], 0, 1)
            send(it, row - 3)

        for v in range(2 * rows, 2 * rows + 3):
            step(it, v)
            send(it, v - 3 - rows)
            forward(it, v - 2 * rows)

        @pl.loop(3, rows)
        def _(row):
            forward(it, row)

    it = ITERS - 1

    @pl.loop(0, rows)
    def _(row):
        arrive(it, row)
        done = before[it, row] + sent[it, row]
        for half in range(halves):
            here_rows = pl.ds(row, planes, stride=rows)
            final[half, here_rows, :] = (
                start[half, here_rows, :] + done[half * planes : (half + 1) * planes]
            )

    for half in range(halves):
        out_ref[:, half * LANES : (half + 1) * LANES] = final[half]

    for it in range(ITERS):
        @pl.loop(0, rows)
        def _(row):
            @pl.loop(1, quad)
            def _(k):
                quad_copy(it, row, k).wait_send()

            @pl.loop(1, levels - level)
            def _(k):
                level_copy(it, row, k).wait_send()


def scoped(n, quad, dims, *refs):
    channels, frames, rows, width, hid, blocks = dims
    strip = width // STRIPS
    packed = lambda *shape: pltpu.VMEM(shape, jnp.bfloat16)
    pl.run_scoped(
        functools.partial(kernel, n, quad, dims, *refs),
        packed(frames, rows, strip, STRIPS, hid),
        packed(frames, rows, strip, STRIPS, hid),
        packed(frames, rows, strip, STRIPS, hid),
        packed(frames, rows + 2, strip + 2, STRIPS, hid),
        packed(frames, rows + 2, strip + 2, STRIPS, hid),
        packed(frames, strip, STRIPS, hid),
        packed(frames, strip, STRIPS, hid),
        packed((strip + 2) * STRIPS, width),
        packed(blocks, 12, STRIPS, hid),
        packed(blocks, 2 * hid, 2 * hid),
        packed(2 * hid, 2 * hid),
        packed(LANES, frames * hid),
        packed(2 * TILE, frames * hid),
    )


def shards(start_frames, plan, noise, w_lift, w_time, spatial, temporal, w_point, w_out):
    n = lax.axis_size("tm")
    channels, frames, rows, width = start_frames.shape
    hid = w_time.shape[0]
    blocks = spatial.shape[0]
    halves = width // LANES
    planes = channels * frames
    quad = max(k for k in range(1, n + 1) if n % k == 0 and k * k <= n)
    flat = (planes * rows, width)
    hbm = pl.BlockSpec(memory_space=pl.ANY)
    f32, bf16 = jnp.float32, jnp.bfloat16
    line = pltpu.VMEM((ITERS, rows, halves * planes, LANES), f32)
    by_half = pltpu.VMEM((halves, planes * rows, LANES), f32)
    result = pl.pallas_call(
        functools.partial(scoped, n, quad, (channels, frames, rows, width, hid, blocks)),
        out_shape=jax.ShapeDtypeStruct(flat, f32),
        in_specs=[pl.BlockSpec(memory_space=pltpu.SMEM)] + [hbm] * 8,
        out_specs=pl.BlockSpec(memory_space=pltpu.VMEM),
        scratch_shapes=[
            by_half,
            by_half,
            pltpu.VMEM((channels, hid), f32),
            pltpu.VMEM((hid, hid), f32),
            pltpu.VMEM((9, blocks, hid), f32),
            pltpu.VMEM((3, blocks, hid), f32),
            pltpu.VMEM((blocks, hid, hid), bf16),
            pltpu.VMEM((channels, hid), f32),
            pltpu.VMEM((LANES, frames * hid), f32),
            pltpu.VMEM((2 * TILE, frames * hid), f32),
            pltpu.VMEM((rows, TILE, width), f32),
            line,
            pltpu.VMEM((ITERS, rows, quad, halves * planes, LANES), f32),
            line,
            pltpu.VMEM((ITERS, rows, n // quad, halves * planes, LANES), f32),
            line,
            by_half,
            pltpu.SemaphoreType.DMA((2 * halves + 6,)),
            pltpu.SemaphoreType.DMA((ITERS, rows, quad + n // quad)),
            pltpu.SemaphoreType.DMA((ITERS, rows, quad + n // quad)),
        ],
        compiler_params=pltpu.CompilerParams(
            collective_id=0, has_side_effects=True, vmem_limit_bytes=62 * 2**20
        ),
    )(
        plan, start_frames.reshape(flat), noise.reshape(flat), w_lift, w_time,
        spatial.transpose(2, 0, 1), temporal.transpose(2, 0, 1), w_point, w_out.T,
    )
    return result.reshape((1,) + start_frames.shape)


def solution(mesh):
    in_specs = (
        P("groups", None, None, None),
        P(("groups", "tm")),
        P("tm", "groups", None, None, None),
        P(),
        P(),
        P(),
        P(),
        P(),
        P(),
    )
    out_specs = P("tm", "groups", None, None, None)
    return jax.shard_map(shards, mesh=mesh, in_specs=in_specs, out_specs=out_specs, check_vma=False)
```

```python
import functools
import math

import jax
import jax.numpy as jnp
from jax import lax
from jax.experimental import pallas as pl
from jax.experimental.pallas import tpu as pltpu
from jax.sharding import PartitionSpec as P

ITERS = 2
NOISE_SCALE = 2.0
MESH = pl.DeviceIdType.MESH
LANES = 128
STRIPS = 16
TILE = 16
WAIT = 5
NT = (((1,), (1,)), ((), ()))


def split_bf16(value):
    high = value.astype(jnp.bfloat16)
    return high, (value - high.astype(jnp.float32)).astype(jnp.bfloat16)


def kernel(
    n, quad, dims,
    plan_ref, start_hbm, noise_hbm, lift_hbm, time_hbm, spatial_hbm, temporal_hbm, point_hbm, wout_hbm,
    out_ref,
    start, noise, lift_in, time_in, spatial_in, temporal_in, point_in, wout_in,
    lift_w, out_w, state, near, far, before, final,
    in_sem, send_sem, recv_sem,
    feat_a, feat_b, last, time_a, time_b, pend, normed, place, taps, point_w, mean_w, lift_b, out_b,
):
    channels, frames, rows, width, hid, blocks = dims
    halves = width // LANES
    planes = channels * frames
    strip = width // STRIPS
    cells = strip * STRIPS
    levels = n // quad
    step_size = 1.0 / n
    bf16 = jnp.bfloat16
    me = lax.axis_index("tm")
    level, member = lax.div(me, quad), lax.rem(me, quad)

    loads = [
        (start_hbm.at[:, pl.ds(half * LANES, LANES)], start.at[half]) for half in range(halves)
    ]
    loads += [(lift_hbm, lift_in), (time_hbm, time_in), (spatial_hbm, spatial_in)]
    loads += [(temporal_hbm, temporal_in), (point_hbm, point_in), (wout_hbm, wout_in)]
    loads += [
        (noise_hbm.at[:, pl.ds(half * LANES, LANES)], noise.at[half]) for half in range(halves)
    ]
    loads = [
        pltpu.make_async_copy(source, target, in_sem.at[k])
        for k, (source, target) in enumerate(loads)
    ]
    for load in loads:
        load.start()

    barrier = pltpu.get_barrier_semaphore()

    @pl.loop(1, n)
    def _(k):
        pl.semaphore_signal(
            barrier, inc=1, device_id={"tm": lax.rem(me + k, n)}, device_id_type=MESH
        )

    for feat in (time_a, time_b):
        for frame in range(frames):
            for row in (0, rows + 1):
                feat[frame, row] = jnp.zeros((strip + 2, STRIPS, hid), bf16)
    spot = lax.broadcasted_iota(jnp.int32, ((strip + 2) * STRIPS, width), 0)
    column = lax.broadcasted_iota(jnp.int32, ((strip + 2) * STRIPS, width), 1)
    wanted = lax.rem(spot, STRIPS) * strip + lax.div(spot, STRIPS) - 1
    place[...] = jnp.where(column == wanted, 1.0, 0.0).astype(bf16)
    one_row = lax.broadcasted_iota(jnp.int32, (rows, TILE, width), 1) == planes
    state[...] = jnp.where(one_row, 1.0, 0.0)
    lift_w[...] = jnp.zeros_like(lift_w)
    out_w[...] = jnp.zeros_like(out_w)
    mean_w[...] = jnp.zeros_like(mean_w)
    point_w[...] = jnp.zeros_like(point_w)
    for out in range(2):
        here = slice(out * hid, (out + 1) * hid)
        mean_w[here, here] = jnp.full((hid, hid), 4.0 / hid, bf16)

    lane = lax.broadcasted_iota(jnp.int32, (8, hid), 1)
    half_hid = hid // 2
    index = lax.rem(lane, half_hid).astype(jnp.float32)
    angles = plan_ref[0].astype(jnp.float32) * jnp.exp(-math.log(1000.0) * index / half_hid)
    embedded = jnp.where(lane < half_hid, jnp.sin(angles), jnp.cos(angles))

    for load in loads:
        load.wait()

    bias = jnp.dot(
        embedded, time_in[...], precision=lax.Precision.HIGHEST, preferred_element_type=jnp.float32
    )[0:1]

    def split_rows(rows_value):
        high = rows_value.astype(bf16).astype(jnp.float32)
        return high, rows_value - high

    bias_high, bias_low = split_rows(bias)
    lift_high, lift_low = split_rows(lift_in[...])
    out_high, out_low = split_rows(wout_in[...])
    for frame in range(frames):
        here = slice(frame * hid, (frame + 1) * hid)
        for channel in range(channels):
            k = channel * frames + frame
            lift_w[k : k + 1, here] = lift_high[channel : channel + 1]
            lift_w[TILE + k : TILE + k + 1, here] = lift_high[channel : channel + 1]
            lift_w[2 * TILE + k : 2 * TILE + k + 1, here] = lift_low[channel : channel + 1]
            out_w[k : k + 1, here] = out_high[channel : channel + 1]
            out_w[TILE + k : TILE + k + 1, here] = out_low[channel : channel + 1]
        lift_w[planes : planes + 1, here] = bias_high
        lift_w[2 * TILE + planes : 2 * TILE + planes + 1, here] = bias_low
    lift_b[...] = lift_w[...].astype(bf16)
    out_b[...] = out_w[...].astype(bf16)
    for block in range(blocks):
        for out in range(2):
            here = slice(out * hid, (out + 1) * hid)
            point_w[block, here, here] = point_in[block]
        for k in range(9):
            weight = spatial_in[k, block : block + 1, :]
            taps[block, k] = jnp.broadcast_to(weight, (STRIPS, hid)).astype(bf16)
        for k in range(3):
            weight = temporal_in[k, block : block + 1, :]
            taps[block, 9 + k] = jnp.broadcast_to(weight, (STRIPS, hid)).astype(bf16)

    def quad_copy(it, row, k):
        return pltpu.make_async_remote_copy(
            src_ref=near.at[it, row, member], dst_ref=near.at[it, row, member],
            send_sem=send_sem.at[k - 1], recv_sem=recv_sem.at[it, row, 0],
            device_id={"tm": level * quad + lax.rem(member + k, quad)}, device_id_type=MESH,
        )

    def level_copy(it, row, k):
        return pltpu.make_async_remote_copy(
            src_ref=far.at[it, row, level], dst_ref=far.at[it, row, level],
            send_sem=send_sem.at[quad + k - 2], recv_sem=recv_sem.at[it, row, 1 + level],
            device_id={"tm": me + k * quad}, device_id_type=MESH,
        )

    def level_from(it, row, lower):
        return pltpu.make_async_remote_copy(
            src_ref=far.at[it, row, lower], dst_ref=far.at[it, row, lower],
            send_sem=send_sem.at[0], recv_sem=recv_sem.at[it, row, 1 + lower],
            device_id={"tm": lower * quad + member}, device_id_type=MESH,
        )

    def quad_from(it, row):
        others = pl.ds(0, quad - 1)
        return pltpu.make_async_remote_copy(
            src_ref=near.at[it, row, others], dst_ref=near.at[it, row, others],
            send_sem=send_sem.at[0], recv_sem=recv_sem.at[it, row, 0],
            device_id={"tm": me}, device_id_type=MESH,
        )

    def all_sent(ref, k):
        return pltpu.make_async_remote_copy(
            src_ref=ref.at[:, :, 0], dst_ref=ref.at[:, :, 0],
            send_sem=send_sem.at[k], recv_sem=recv_sem.at[0, 0, 0],
            device_id={"tm": me}, device_id_type=MESH,
        )

    def send(it, row):
        for k in range(1, quad):
            quad_copy(it, row, k).start()

    def forward(it, row):
        quad_from(it, row).wait_recv()
        zero = jnp.zeros((halves * planes, LANES), jnp.float32)
        everything, prefix = zero, zero
        for k in range(quad):
            part = near[it, row, k]
            everything = everything + part
            prefix = prefix + jnp.where(k < member, part, 0.0)
        far[it, row, level] = everything
        before[it, row] = prefix

        @pl.loop(1, levels - level)
        def _(k):
            level_copy(it, row, k).start()

    def arrive(it, row):
        @pl.loop(0, level)
        def _(lower):
            level_from(it, row, lower).wait_recv()
            before[it, row] += far[it, row, lower]

    def lift(it, row, target, at_row, blend, to_row):
        for half in range(halves):
            now = start[half, pl.ds(row, planes, stride=rows), :]
            if it > 0:
                now = now + before[it - 1, row, half * planes : (half + 1) * planes]
            state[row, 0:planes, half * LANES : (half + 1) * LANES] = now
        high, low = split_bf16(state[row])
        spare = jnp.zeros((LANES - 3 * TILE, width), bf16)
        stack = jnp.concatenate([high, low, high, spare], axis=0)
        turned = lax.dot_general(place[...], stack, NT, preferred_element_type=jnp.float32)
        lifted = jnp.dot(
            turned.astype(bf16), lift_b[...], preferred_element_type=jnp.float32
        ).astype(bf16)
        fresh = [
            lifted[:, frame * hid : (frame + 1) * hid].reshape(strip + 2, STRIPS, hid)
            for frame in range(frames)
        ]
        for frame in range(frames):
            target[frame, at_row] = fresh[frame][1 : strip + 1]
            blend[frame, to_row] = in_time(fresh, frame, 0)

    def in_time(fresh, frame, block):
        mixed = taps[block, 10] * fresh[frame]
        if frame > 0:
            mixed = mixed + taps[block, 9] * fresh[frame - 1]
        if frame + 1 < frames:
            mixed = mixed + taps[block, 11] * fresh[frame + 1]
        return mixed

    def convolve(source, first, block):
        weights = [taps[block, k] for k in range(9)]
        for frame in range(frames):
            for at in range(strip):
                lines = []
                for a in range(3):
                    terms = [weights[3 * a + c] * source[frame, first + a, at + c] for c in range(3)]
                    lines.append(terms[0] + terms[1] + terms[2])
                pend[frame, at] = lines[0] + lines[1] + lines[2]

    def pairs(ref):
        return jnp.concatenate(
            [
                jnp.concatenate([ref[pair + k].reshape(cells, hid) for k in range(2)], axis=1)
                for pair in range(0, frames, 2)
            ],
            axis=0,
        )

    def normalize():
        mixed = pairs(pend)
        mean = jnp.dot(mixed * mixed, mean_w[...], preferred_element_type=jnp.float32)
        scale = lax.rsqrt(mean.astype(bf16) + jnp.bfloat16(4e-06))
        half = mixed * scale
        done = half * jnp.tanh(half) + half
        for frame in range(frames):
            first, side = (frame // 2) * cells, (frame % 2) * hid
            part = done[first : first + cells, side : side + hid]
            normed[frame] = part.reshape(strip, STRIPS, hid)

    def update(source, at_row, target, to_row, block, blend=None, blend_row=None):
        sub = lax.broadcasted_iota(jnp.int32, (STRIPS, hid), 0)
        change = jnp.dot(pairs(normed), point_w[block], preferred_element_type=jnp.float32)
        fresh = []
        for frame in range(frames):
            first, side = (frame // 2) * cells, (frame % 2) * hid
            old = source[frame, at_row].reshape(cells, hid)
            now = old + change[first : first + cells, side : side + hid].astype(bf16)
            fresh.append(now.reshape(strip, STRIPS, hid))
            target[frame, to_row] = fresh[frame]
        if blend is None:
            return
        for frame in range(frames):
            mixed = in_time(fresh, frame, block + 1)
            blend[frame, blend_row, 1 : strip + 1] = mixed
            tail = mixed[strip - 1].astype(jnp.float32)
            tail = jnp.where(sub == 0, 0.0, pltpu.roll(tail, 1, 0))
            blend[frame, blend_row, 0] = tail.astype(bf16)
            head = mixed[0].astype(jnp.float32)
            head = jnp.where(sub == STRIPS - 1, 0.0, pltpu.roll(head, STRIPS - 1, 0))
            blend[frame, blend_row, strip + 1] = head.astype(bf16)

    def output(it, row, source, at_row):
        seen = jnp.concatenate(
            [source[frame, at_row].reshape(cells, hid) for frame in range(frames)], axis=1
        )
        both = lax.dot_general(out_b[...], seen, NT, preferred_element_type=jnp.float32)
        high, low = split_bf16(both[0:TILE] + both[TILE : 2 * TILE])
        turned = jnp.dot(
            jnp.concatenate([high, low], axis=0), place[STRIPS : STRIPS + cells, :],
            preferred_element_type=jnp.float32,
        )
        turned = turned[0:TILE] + turned[TILE : 2 * TILE]
        for half in range(halves):
            drift = (
                step_size * turned[0:planes, half * LANES : (half + 1) * LANES]
                + NOISE_SCALE
                * math.sqrt(step_size)
                * noise[half, pl.ds(row, planes, stride=rows), :]
            )
            near[it, row, member, half * planes : (half + 1) * planes] = drift

    def step(it, v):
        if 0 <= v - 3 - rows < rows:
            output(it, v - 3 - rows, last, v - 3 - rows)
        if 0 <= v - 2 < rows:
            update(feat_a, v - 2, feat_b, v - 2, 0, time_b, v - 1)
        elif rows <= v - 2 < 2 * rows:
            update(feat_b, v - 2 - rows, last, v - 2 - rows, 1)
        if 0 <= v - 1 < 2 * rows:
            normalize()
        if v < rows:
            convolve(time_a, v, 0)
        elif v < 2 * rows:
            convolve(time_b, v - rows, 1)
        if v + 2 < rows:
            lift(it, v + 2, feat_a, v + 2, time_a, v + 3)

    for it in range(ITERS):
        for row in range(2):
            if it > 0:
                arrive(it - 1, row)
            lift(it, row, feat_a, row, time_a, row + 1)
        for v in range(2 * rows + 3):
            if it > 0 and v + 2 < rows:
                arrive(it - 1, v + 2)
            step(it, v)
            done = v - 3 - rows
            if done < 0:
                continue
            if it == 0 and done == 0:
                pl.semaphore_wait(barrier, n - 1)
            send(it, done)
            if done >= WAIT:
                forward(it, done - WAIT)
        for row in range(rows - WAIT, rows):
            forward(it, row)

    it = ITERS - 1

    for row in range(rows):
        arrive(it, row)
        done = before[it, row] + near[it, row, member]
        for half in range(halves):
            places = pl.ds(row, planes, stride=rows)
            final[half, places, :] = (
                start[half, places, :] + done[half * planes : (half + 1) * planes]
            )
    for half in range(halves):
        out_ref[:, half * LANES : (half + 1) * LANES] = final[half]

    for k in range(quad - 1):
        all_sent(near, k).wait_send()

    @pl.loop(1, levels - level)
    def _(k):
        all_sent(far, quad + k - 2).wait_send()


def scoped(n, quad, dims, *refs):
    channels, frames, rows, width, hid, blocks = dims
    strip = width // STRIPS
    packed = lambda *shape: pltpu.VMEM(shape, jnp.bfloat16)
    pl.run_scoped(
        functools.partial(kernel, n, quad, dims, *refs),
        packed(frames, rows, strip, STRIPS, hid),
        packed(frames, rows, strip, STRIPS, hid),
        packed(frames, rows, strip, STRIPS, hid),
        packed(frames, rows + 2, strip + 2, STRIPS, hid),
        packed(frames, rows + 2, strip + 2, STRIPS, hid),
        packed(frames, strip, STRIPS, hid),
        packed(frames, strip, STRIPS, hid),
        packed((strip + 2) * STRIPS, width),
        packed(blocks, 12, STRIPS, hid),
        packed(blocks, 2 * hid, 2 * hid),
        packed(2 * hid, 2 * hid),
        packed(LANES, frames * hid),
        packed(2 * TILE, frames * hid),
    )


def shards(start_frames, plan, noise, w_lift, w_time, spatial, temporal, w_point, w_out):
    n = lax.axis_size("tm")
    channels, frames, rows, width = start_frames.shape
    hid = w_time.shape[0]
    blocks = spatial.shape[0]
    halves = width // LANES
    planes = channels * frames
    quad = max(k for k in range(1, n + 1) if n % k == 0 and k * k <= n)
    flat = (planes * rows, width)
    hbm = pl.BlockSpec(memory_space=pl.ANY)
    f32, bf16 = jnp.float32, jnp.bfloat16
    by_half = pltpu.VMEM((halves, planes * rows, LANES), f32)
    result = pl.pallas_call(
        functools.partial(scoped, n, quad, (channels, frames, rows, width, hid, blocks)),
        out_shape=jax.ShapeDtypeStruct(flat, f32),
        in_specs=[pl.BlockSpec(memory_space=pltpu.SMEM)] + [hbm] * 8,
        out_specs=pl.BlockSpec(memory_space=pltpu.VMEM),
        scratch_shapes=[
            by_half,
            by_half,
            pltpu.VMEM((channels, hid), f32),
            pltpu.VMEM((hid, hid), f32),
            pltpu.VMEM((9, blocks, hid), f32),
            pltpu.VMEM((3, blocks, hid), f32),
            pltpu.VMEM((blocks, hid, hid), bf16),
            pltpu.VMEM((channels, hid), f32),
            pltpu.VMEM((LANES, frames * hid), f32),
            pltpu.VMEM((2 * TILE, frames * hid), f32),
            pltpu.VMEM((rows, TILE, width), f32),
            pltpu.VMEM((ITERS, rows, quad, halves * planes, LANES), f32),
            pltpu.VMEM((ITERS, rows, n // quad, halves * planes, LANES), f32),
            pltpu.VMEM((ITERS, rows, halves * planes, LANES), f32),
            by_half,
            pltpu.SemaphoreType.DMA((2 * halves + 6,)),
            pltpu.SemaphoreType.DMA((quad + n // quad - 2,)),
            pltpu.SemaphoreType.DMA((ITERS, rows, n // quad)),
        ],
        compiler_params=pltpu.CompilerParams(
            collective_id=0, has_side_effects=True, vmem_limit_bytes=62 * 2**20
        ),
    )(
        plan, start_frames.reshape(flat), noise.reshape(flat), w_lift, w_time,
        spatial.transpose(2, 0, 1), temporal.transpose(2, 0, 1), w_point, w_out.T,
    )
    return result.reshape((1,) + start_frames.shape)


def solution(mesh):
    in_specs = (
        P("groups", None, None, None),
        P(("groups", "tm")),
        P("tm", "groups", None, None, None),
        P(),
        P(),
        P(),
        P(),
        P(),
        P(),
    )
    out_specs = P("tm", "groups", None, None, None)
    return jax.shard_map(shards, mesh=mesh, in_specs=in_specs, out_specs=out_specs, check_vma=False)
```

```python
import functools
import math

import jax
import jax.numpy as jnp
from jax import lax
from jax.experimental import pallas as pl
from jax.experimental.pallas import tpu as pltpu
from jax.sharding import PartitionSpec as P

ITERS = 2
NOISE_SCALE = 2.0
MESH = pl.DeviceIdType.MESH
LANES = 128
STRIPS = 16
TILE = 16
WAIT = 5
NT = (((1,), (1,)), ((), ()))


def split_bf16(value):
    high = value.astype(jnp.bfloat16)
    return high, (value - high.astype(jnp.float32)).astype(jnp.bfloat16)


def kernel(
    n, quad, dims,
    plan_ref, start_hbm, noise_hbm, lift_hbm, time_hbm, spatial_hbm, temporal_hbm, point_hbm, wout_hbm,
    out_ref,
    start, noise, lift_in, time_in, spatial_in, temporal_in, point_in, wout_in,
    lift_w, out_w, state, near, far, before, final,
    in_sem, send_sem, recv_sem,
    feat_a, feat_b, last, time_a, time_b, pend, normed, place, taps, point_w, mean_w, lift_b, out_b,
):
    channels, frames, rows, width, hid, blocks = dims
    halves = width // LANES
    planes = channels * frames
    strip = width // STRIPS
    cells = strip * STRIPS
    levels = n // quad
    step_size = 1.0 / n
    bf16 = jnp.bfloat16
    me = lax.axis_index("tm")
    level, member = lax.div(me, quad), lax.rem(me, quad)

    loads = [
        (start_hbm.at[:, pl.ds(half * LANES, LANES)], start.at[half]) for half in range(halves)
    ]
    loads += [(lift_hbm, lift_in), (time_hbm, time_in), (spatial_hbm, spatial_in)]
    loads += [(temporal_hbm, temporal_in), (point_hbm, point_in), (wout_hbm, wout_in)]
    loads += [
        (noise_hbm.at[:, pl.ds(half * LANES, LANES)], noise.at[half]) for half in range(halves)
    ]
    loads = [
        pltpu.make_async_copy(source, target, in_sem.at[k])
        for k, (source, target) in enumerate(loads)
    ]
    for load in loads:
        load.start()

    barrier = pltpu.get_barrier_semaphore()

    @pl.loop(1, n)
    def _(k):
        pl.semaphore_signal(
            barrier, inc=1, device_id={"tm": lax.rem(me + k, n)}, device_id_type=MESH
        )

    for feat in (time_a, time_b):
        for frame in range(frames):
            for row in (0, rows + 1):
                feat[frame, row] = jnp.zeros((strip + 2, STRIPS, hid), bf16)
    spot = lax.broadcasted_iota(jnp.int32, ((strip + 2) * STRIPS, width), 0)
    column = lax.broadcasted_iota(jnp.int32, ((strip + 2) * STRIPS, width), 1)
    wanted = lax.rem(spot, STRIPS) * strip + lax.div(spot, STRIPS) - 1
    place[...] = jnp.where(column == wanted, 1.0, 0.0).astype(bf16)
    one_row = lax.broadcasted_iota(jnp.int32, (rows, TILE, width), 1) == planes
    state[...] = jnp.where(one_row, 1.0, 0.0)
    lift_w[...] = jnp.zeros_like(lift_w)
    out_w[...] = jnp.zeros_like(out_w)
    mean_w[...] = jnp.zeros_like(mean_w)
    point_w[...] = jnp.zeros_like(point_w)
    for out in range(2):
        here = slice(out * hid, (out + 1) * hid)
        mean_w[here, here] = jnp.full((hid, hid), 4.0 / hid, bf16)

    lane = lax.broadcasted_iota(jnp.int32, (8, hid), 1)
    half_hid = hid // 2
    index = lax.rem(lane, half_hid).astype(jnp.float32)
    angles = plan_ref[0].astype(jnp.float32) * jnp.exp(-math.log(1000.0) * index / half_hid)
    embedded = jnp.where(lane < half_hid, jnp.sin(angles), jnp.cos(angles))

    for load in loads:
        load.wait()

    bias = jnp.dot(
        embedded, time_in[...], precision=lax.Precision.HIGHEST, preferred_element_type=jnp.float32
    )[0:1]

    def split_rows(rows_value):
        high = rows_value.astype(bf16).astype(jnp.float32)
        return high, rows_value - high

    bias_high, bias_low = split_rows(bias)
    lift_high, lift_low = split_rows(lift_in[...])
    out_high, out_low = split_rows(wout_in[...])
    for frame in range(frames):
        here = slice(frame * hid, (frame + 1) * hid)
        for channel in range(channels):
            k = channel * frames + frame
            lift_w[k : k + 1, here] = lift_high[channel : channel + 1]
            lift_w[TILE + k : TILE + k + 1, here] = lift_high[channel : channel + 1]
            lift_w[2 * TILE + k : 2 * TILE + k + 1, here] = lift_low[channel : channel + 1]
            out_w[k : k + 1, here] = out_high[channel : channel + 1]
            out_w[TILE + k : TILE + k + 1, here] = out_low[channel : channel + 1]
        lift_w[planes : planes + 1, here] = bias_high
        lift_w[2 * TILE + planes : 2 * TILE + planes + 1, here] = bias_low
    lift_b[...] = lift_w[...].astype(bf16)
    out_b[...] = out_w[...].astype(bf16)
    for block in range(blocks):
        for out in range(2):
            here = slice(out * hid, (out + 1) * hid)
            point_w[block, here, here] = point_in[block]
        for k in range(9):
            weight = spatial_in[k, block : block + 1, :]
            taps[block, k] = jnp.broadcast_to(weight, (STRIPS, hid)).astype(bf16)
        for k in range(3):
            weight = temporal_in[k, block : block + 1, :]
            taps[block, 9 + k] = jnp.broadcast_to(weight, (STRIPS, hid)).astype(bf16)

    def quad_copy(it, row, k):
        return pltpu.make_async_remote_copy(
            src_ref=near.at[it, row, member], dst_ref=near.at[it, row, member],
            send_sem=send_sem.at[k - 1], recv_sem=recv_sem.at[it, row, 0],
            device_id={"tm": level * quad + lax.rem(member + k, quad)}, device_id_type=MESH,
        )

    def level_copy(it, row, k):
        return pltpu.make_async_remote_copy(
            src_ref=far.at[it, row, level], dst_ref=far.at[it, row, level],
            send_sem=send_sem.at[quad + k - 2], recv_sem=recv_sem.at[it, row, 1 + level],
            device_id={"tm": me + k * quad}, device_id_type=MESH,
        )

    def level_from(it, row, lower):
        return pltpu.make_async_remote_copy(
            src_ref=far.at[it, row, lower], dst_ref=far.at[it, row, lower],
            send_sem=send_sem.at[0], recv_sem=recv_sem.at[it, row, 1 + lower],
            device_id={"tm": lower * quad + member}, device_id_type=MESH,
        )

    def quad_from(it, row):
        others = pl.ds(0, quad - 1)
        return pltpu.make_async_remote_copy(
            src_ref=near.at[it, row, others], dst_ref=near.at[it, row, others],
            send_sem=send_sem.at[0], recv_sem=recv_sem.at[it, row, 0],
            device_id={"tm": me}, device_id_type=MESH,
        )

    def all_sent(ref, k):
        return pltpu.make_async_remote_copy(
            src_ref=ref.at[:, :, 0], dst_ref=ref.at[:, :, 0],
            send_sem=send_sem.at[k], recv_sem=recv_sem.at[0, 0, 0],
            device_id={"tm": me}, device_id_type=MESH,
        )

    def send(it, row):
        for k in range(1, quad):
            quad_copy(it, row, k).start()

    def forward(it, row):
        quad_from(it, row).wait_recv()
        zero = jnp.zeros((halves * planes, LANES), jnp.float32)
        everything, prefix = zero, zero
        for k in range(quad):
            part = near[it, row, k]
            everything = everything + part
            prefix = prefix + jnp.where(k < member, part, 0.0)
        far[it, row, level] = everything
        before[it, row] = prefix

        @pl.loop(1, levels - level)
        def _(k):
            level_copy(it, row, k).start()

    def arrive(it, row):
        @pl.loop(0, level)
        def _(lower):
            level_from(it, row, lower).wait_recv()
            before[it, row] += far[it, row, lower]

    def lift(it, row, target, at_row, blend, to_row):
        for half in range(halves):
            now = start[half, pl.ds(row, planes, stride=rows), :]
            if it > 0:
                now = now + before[it - 1, row, half * planes : (half + 1) * planes]
            state[row, 0:planes, half * LANES : (half + 1) * LANES] = now
        high, low = split_bf16(state[row])
        spare = jnp.zeros((LANES - 3 * TILE, width), bf16)
        stack = jnp.concatenate([high, low, high, spare], axis=0)
        turned = lax.dot_general(place[...], stack, NT, preferred_element_type=jnp.float32)
        lifted = jnp.dot(
            turned.astype(bf16), lift_b[...], preferred_element_type=jnp.float32
        ).astype(bf16)
        fresh = [
            lifted[:, frame * hid : (frame + 1) * hid].reshape(strip + 2, STRIPS, hid)
            for frame in range(frames)
        ]
        for frame in range(frames):
            target[frame, at_row] = fresh[frame][1 : strip + 1]
            blend[frame, to_row] = in_time(fresh, frame, 0)

    def in_time(fresh, frame, block):
        mixed = taps[block, 10] * fresh[frame]
        if frame > 0:
            mixed = mixed + taps[block, 9] * fresh[frame - 1]
        if frame + 1 < frames:
            mixed = mixed + taps[block, 11] * fresh[frame + 1]
        return mixed

    def convolve(source, first, block):
        weights = [taps[block, k] for k in range(9)]
        for frame in range(frames):
            for at in range(strip):
                lines = []
                for a in range(3):
                    terms = [weights[3 * a + c] * source[frame, first + a, at + c] for c in range(3)]
                    lines.append(terms[0] + terms[1] + terms[2])
                pend[frame, at] = lines[0] + lines[1] + lines[2]

    def pairs(ref):
        return jnp.concatenate(
            [
                jnp.concatenate([ref[pair + k].reshape(cells, hid) for k in range(2)], axis=1)
                for pair in range(0, frames, 2)
            ],
            axis=0,
        )

    def normalize():
        mixed = pairs(pend)
        mean = jnp.dot(mixed * mixed, mean_w[...], preferred_element_type=jnp.float32)
        scale = lax.rsqrt(mean.astype(bf16) + jnp.bfloat16(4e-06))
        half = mixed * scale
        done = half * jnp.tanh(half) + half
        for frame in range(frames):
            first, side = (frame // 2) * cells, (frame % 2) * hid
            part = done[first : first + cells, side : side + hid]
            normed[frame] = part.reshape(strip, STRIPS, hid)

    def update(source, at_row, target, to_row, block, blend=None, blend_row=None):
        sub = lax.broadcasted_iota(jnp.int32, (STRIPS, hid), 0)
        change = jnp.dot(pairs(normed), point_w[block], preferred_element_type=jnp.float32)
        fresh = []
        for frame in range(frames):
            first, side = (frame // 2) * cells, (frame % 2) * hid
            old = source[frame, at_row].reshape(cells, hid)
            now = old + change[first : first + cells, side : side + hid].astype(bf16)
            fresh.append(now.reshape(strip, STRIPS, hid))
            target[frame, to_row] = fresh[frame]
        if blend is None:
            return
        for frame in range(frames):
            mixed = in_time(fresh, frame, block + 1)
            blend[frame, blend_row, 1 : strip + 1] = mixed
            tail = mixed[strip - 1].astype(jnp.float32)
            tail = jnp.where(sub == 0, 0.0, pltpu.roll(tail, 1, 0))
            blend[frame, blend_row, 0] = tail.astype(bf16)
            head = mixed[0].astype(jnp.float32)
            head = jnp.where(sub == STRIPS - 1, 0.0, pltpu.roll(head, STRIPS - 1, 0))
            blend[frame, blend_row, strip + 1] = head.astype(bf16)

    def output(it, row, source, at_row):
        seen = jnp.concatenate(
            [source[frame, at_row].reshape(cells, hid) for frame in range(frames)], axis=1
        )
        both = lax.dot_general(out_b[...], seen, NT, preferred_element_type=jnp.float32)
        high, low = split_bf16(both[0:TILE] + both[TILE : 2 * TILE])
        turned = jnp.dot(
            jnp.concatenate([high, low], axis=0), place[STRIPS : STRIPS + cells, :],
            preferred_element_type=jnp.float32,
        )
        turned = turned[0:TILE] + turned[TILE : 2 * TILE]
        for half in range(halves):
            drift = (
                step_size * turned[0:planes, half * LANES : (half + 1) * LANES]
                + NOISE_SCALE
                * math.sqrt(step_size)
                * noise[half, pl.ds(row, planes, stride=rows), :]
            )
            near[it, row, member, half * planes : (half + 1) * planes] = drift

    def step(it, v):
        if 0 <= v - 3 - rows < rows:
            output(it, v - 3 - rows, last, v - 3 - rows)
        if 0 <= v - 2 < rows:
            update(feat_a, v - 2, feat_b, v - 2, 0, time_b, v - 1)
        elif rows <= v - 2 < 2 * rows:
            update(feat_b, v - 2 - rows, last, v - 2 - rows, 1)
        if 0 <= v - 1 < 2 * rows:
            normalize()
        if v < rows:
            convolve(time_a, v, 0)
        elif v < 2 * rows:
            convolve(time_b, v - rows, 1)
        if v + 2 < rows:
            lift(it, v + 2, feat_a, v + 2, time_a, v + 3)

    for it in range(ITERS):
        wait = WAIT if it + 1 < ITERS else rows
        for row in range(2):
            if it > 0:
                arrive(it - 1, row)
            lift(it, row, feat_a, row, time_a, row + 1)
        for v in range(2 * rows + 3):
            if it > 0 and v + 2 < rows:
                arrive(it - 1, v + 2)
            step(it, v)
            done = v - 3 - rows
            if done < 0:
                continue
            if it == 0 and done == 0:
                pl.semaphore_wait(barrier, n - 1)
            send(it, done)
            if done >= wait:
                forward(it, done - wait)
        for row in range(rows - wait, rows):
            forward(it, row)

    it = ITERS - 1

    for row in range(rows):
        arrive(it, row)
        done = before[it, row] + near[it, row, member]
        for half in range(halves):
            places = pl.ds(row, planes, stride=rows)
            final[half, places, :] = (
                start[half, places, :] + done[half * planes : (half + 1) * planes]
            )
    for half in range(halves):
        out_ref[:, half * LANES : (half + 1) * LANES] = final[half]

    for k in range(quad - 1):
        all_sent(near, k).wait_send()

    @pl.loop(1, levels - level)
    def _(k):
        all_sent(far, quad + k - 2).wait_send()


def scoped(n, quad, dims, *refs):
    channels, frames, rows, width, hid, blocks = dims
    strip = width // STRIPS
    packed = lambda *shape: pltpu.VMEM(shape, jnp.bfloat16)
    pl.run_scoped(
        functools.partial(kernel, n, quad, dims, *refs),
        packed(frames, rows, strip, STRIPS, hid),
        packed(frames, rows, strip, STRIPS, hid),
        packed(frames, rows, strip, STRIPS, hid),
        packed(frames, rows + 2, strip + 2, STRIPS, hid),
        packed(frames, rows + 2, strip + 2, STRIPS, hid),
        packed(frames, strip, STRIPS, hid),
        packed(frames, strip, STRIPS, hid),
        packed((strip + 2) * STRIPS, width),
        packed(blocks, 12, STRIPS, hid),
        packed(blocks, 2 * hid, 2 * hid),
        packed(2 * hid, 2 * hid),
        packed(LANES, frames * hid),
        packed(2 * TILE, frames * hid),
    )


def shards(start_frames, plan, noise, w_lift, w_time, spatial, temporal, w_point, w_out):
    n = lax.axis_size("tm")
    channels, frames, rows, width = start_frames.shape
    hid = w_time.shape[0]
    blocks = spatial.shape[0]
    halves = width // LANES
    planes = channels * frames
    quad = max(k for k in range(1, n + 1) if n % k == 0 and k * k <= n)
    flat = (planes * rows, width)
    hbm = pl.BlockSpec(memory_space=pl.ANY)
    f32, bf16 = jnp.float32, jnp.bfloat16
    by_half = pltpu.VMEM((halves, planes * rows, LANES), f32)
    result = pl.pallas_call(
        functools.partial(scoped, n, quad, (channels, frames, rows, width, hid, blocks)),
        out_shape=jax.ShapeDtypeStruct(flat, f32),
        in_specs=[pl.BlockSpec(memory_space=pltpu.SMEM)] + [hbm] * 8,
        out_specs=pl.BlockSpec(memory_space=pltpu.VMEM),
        scratch_shapes=[
            by_half,
            by_half,
            pltpu.VMEM((channels, hid), f32),
            pltpu.VMEM((hid, hid), f32),
            pltpu.VMEM((9, blocks, hid), f32),
            pltpu.VMEM((3, blocks, hid), f32),
            pltpu.VMEM((blocks, hid, hid), bf16),
            pltpu.VMEM((channels, hid), f32),
            pltpu.VMEM((LANES, frames * hid), f32),
            pltpu.VMEM((2 * TILE, frames * hid), f32),
            pltpu.VMEM((rows, TILE, width), f32),
            pltpu.VMEM((ITERS, rows, quad, halves * planes, LANES), f32),
            pltpu.VMEM((ITERS, rows, n // quad, halves * planes, LANES), f32),
            pltpu.VMEM((ITERS, rows, halves * planes, LANES), f32),
            by_half,
            pltpu.SemaphoreType.DMA((2 * halves + 6,)),
            pltpu.SemaphoreType.DMA((quad + n // quad - 2,)),
            pltpu.SemaphoreType.DMA((ITERS, rows, n // quad)),
        ],
        compiler_params=pltpu.CompilerParams(
            collective_id=0, has_side_effects=True, vmem_limit_bytes=62 * 2**20
        ),
    )(
        plan, start_frames.reshape(flat), noise.reshape(flat), w_lift, w_time,
        spatial.transpose(2, 0, 1), temporal.transpose(2, 0, 1), w_point, w_out.T,
    )
    return result.reshape((1,) + start_frames.shape)


def solution(mesh):
    in_specs = (
        P("groups", None, None, None),
        P(("groups", "tm")),
        P("tm", "groups", None, None, None),
        P(),
        P(),
        P(),
        P(),
        P(),
        P(),
    )
    out_specs = P("tm", "groups", None, None, None)
    return jax.shard_map(shards, mesh=mesh, in_specs=in_specs, out_specs=out_specs, check_vma=False)
```
